32 devices in a mesh: tm: 8 (over y, x, core), space: 4 (over z).
Axes of the slice: x: 2, y: 2, z: 4, core: 2. Of those that a mesh axis runs over, the one named last changes fastest.
Arguments:
- start_state: float32 [6, 2048], P(None, 'space'), may hold values from -6 to 6, as said below
- fine_nodes: float32 [8, 3, 6, 2048], P('tm', None, None, 'space'), may hold values from -8 to 8, as said below
Outputs:
- new_places: float32 [8, 3, 3, 2048], P('tm', None, None, 'space')
- new_strengths: float32 [8, 3, 3, 2048], P('tm', None, None, 'space')
- next_places: float32 [8, 3, 2048], P('tm', None, 'space')
- next_strengths: float32 [8, 3, 2048], P('tm', None, 'space')
The draws below stay inside these ranges and needn't reach their ends.
Inputs may be any that keep to these rules, and one draw needn't show every extreme that they name: `start_state`: rows 0 to 2 are positions within the box from -0.5 to 0.5 give or take 0.05; the particles are numbered along a Morton (Z-order) curve of the box, so that runs of consecutive particles lie close together. `fine_nodes`: rows 0 to 2 are positions within the box from -0.5 to 0.5 give or take 0.1, numbered along the same Morton curve as start_state.
All inputs are finite; a program needn't handle non-finite values.
Results may differ from the reference program's by a relative error of at most 0.0003.
Values sent between devices are 32-bit elements; how exact they have to be, the bound alone decides.
A program may use at most 64 MiB of HBM per device.

```python
import math
import jax
import jax.numpy as jnp
from jax import lax

CLUSTER = 16
PARTICLES = 2048
SLICES = 8


def cell_coordinate(particle_index, dimension, total_bits):
    coordinate = jnp.zeros_like(particle_index)
    depth_level = 0
    for bit_place in range(dimension, total_bits, 3):
        bit_value = jnp.bitwise_and(jnp.right_shift(particle_index, bit_place), 1)
        coordinate = coordinate + jnp.left_shift(bit_value, depth_level)
        depth_level = depth_level + 1
    return (coordinate, depth_level)


def morton_places(key):
    particle_index = jnp.arange(PARTICLES, dtype=jnp.int32)
    total_bits = max(3, (PARTICLES - 1).bit_length())
    jitter = jax.random.uniform(key, (3, PARTICLES), jnp.float32)
    rows_out = []
    for dimension in range(3):
        coordinate, depth_level = cell_coordinate(particle_index, dimension, total_bits)
        rows_out.append((coordinate.astype(jnp.float32) + jitter[dimension]) / float(2 ** depth_level) - 0.5)
    return jnp.stack(rows_out)


def base_draw(key):
    keys = jax.random.split(jax.random.fold_in(key, 7), 2)
    places = morton_places(keys[0])
    strengths = jnp.clip(jax.random.normal(keys[1], (3, PARTICLES), jnp.float32), -4.0, 4.0)
    return (places, strengths)


def draw_start_state(key, part):
    places, strengths = base_draw(key)
    return jnp.concatenate([places, strengths], axis=0)


def draw_fine_nodes(key, part):
    places, strengths = base_draw(key)
    keys = jax.random.split(jax.random.fold_in(key, 13), 2)
    drift = jnp.clip(0.02 * jax.random.normal(keys[0], (SLICES, 3, 3, PARTICLES), jnp.float32), -0.1, 0.1)
    ratio = 1.0 + jnp.clip(0.1 * jax.random.normal(keys[1], (SLICES, 3, 3, PARTICLES), jnp.float32), -0.3, 0.3)
    positions = places[None, None] + drift
    moments = strengths[None, None] * ratio
    return jnp.concatenate([positions, moments], axis=2)


def setup_inputs(seed: int = 0) -> dict:
    seeds = jax.random.split(jax.random.key(seed), 3)
    return {
        "start_state": draw_start_state(jax.random.fold_in(seeds[2], 71), 0),
        "fine_nodes": draw_fine_nodes(jax.random.fold_in(seeds[2], 71), 0),
    }


core_squared = 0.01
step_length = 0.02

def cross_rows(left, right):
    return jnp.stack([left[1] * right[2] - left[2] * right[1], left[2] * right[0] - left[0] * right[2], left[0] * right[1] - left[1] * right[0]])

def tile_sums(totals, target, source):
    gap_x = target[0][:, None] - source[0][None, :]
    gap_y = target[1][:, None] - source[1][None, :]
    gap_z = target[2][:, None] - source[2][None, :]
    spread = gap_x * gap_x + gap_y * gap_y + gap_z * gap_z + core_squared
    inverse = lax.rsqrt(spread)
    factor = inverse * inverse * inverse
    steep = 3.0 * factor * inverse * inverse
    curl_x = gap_y * source[5][None, :] - gap_z * source[4][None, :]
    curl_y = gap_z * source[3][None, :] - gap_x * source[5][None, :]
    curl_z = gap_x * source[4][None, :] - gap_y * source[3][None, :]
    along = steep * (target[3][:, None] * gap_x + target[4][:, None] * gap_y + target[5][:, None] * gap_z)
    velocity = jnp.stack([lax.optimization_barrier(jnp.sum(factor * curl_x, axis=1)), lax.optimization_barrier(jnp.sum(factor * curl_y, axis=1)), lax.optimization_barrier(jnp.sum(factor * curl_z, axis=1))])
    weighted = jnp.stack([lax.optimization_barrier(jnp.sum(factor * source[3][None, :], axis=1)), lax.optimization_barrier(jnp.sum(factor * source[4][None, :], axis=1)), lax.optimization_barrier(jnp.sum(factor * source[5][None, :], axis=1))])
    stretch = jnp.stack([lax.optimization_barrier(jnp.sum(along * curl_x, axis=1)), lax.optimization_barrier(jnp.sum(along * curl_y, axis=1)), lax.optimization_barrier(jnp.sum(along * curl_z, axis=1))])
    return (totals[0] + velocity, totals[1] + weighted, totals[2] + stretch)

def block_sums(totals, target, source):
    length = source.shape[1]
    block_len = math.gcd(length, 512)
    if length == block_len:
        return tile_sums(totals, target, source)
    blocks = source.reshape(6, length // block_len, block_len).transpose(1, 0, 2)

    def scan_step(carry, block):
        return (tile_sums(carry, target, block), None)
    totals, unused = lax.scan(scan_step, totals, blocks)
    return totals

def empty_sums(target):
    zeros = jnp.zeros((3, target.shape[1]), jnp.float32)
    return (zeros, zeros, zeros)

def finish(totals, target, coupling):
    stretch = cross_rows(target[3:6], totals[1]) - totals[2]
    return -coupling * jnp.concatenate([totals[0], stretch], axis=0)

def aggregate(state):
    grouped = state.reshape(6, state.shape[1] // CLUSTER, CLUSTER)
    return jnp.concatenate([lax.optimization_barrier(jnp.mean(grouped[0:3], axis=2)), lax.optimization_barrier(jnp.sum(grouped[3:6], axis=2))], axis=0)

def reference(start_state, fine_nodes):
    coupling = 1.0 / (4.0 * math.pi * math.sqrt(PARTICLES))

    def evaluate(target, source):
        return finish(block_sums(empty_sums(target), target, source), target, coupling)

    def first_pass(node_states):
        fine_first = evaluate(node_states[0], node_states[0])
        fine_middle = evaluate(node_states[1], node_states[1])
        fine_last = evaluate(node_states[2], node_states[2])
        coarse_first = evaluate(node_states[0], aggregate(node_states[0]))
        coarse_last = evaluate(node_states[2], aggregate(node_states[2]))
        correction = step_length * ((fine_first + 4.0 * fine_middle + fine_last) / 6.0 - 0.5 * (coarse_first + coarse_last))
        return (jnp.stack([fine_first, fine_middle, fine_last]), coarse_first, coarse_last, correction)
    fine_values, coarse_firsts, coarse_lasts, corrections = lax.map(first_pass, fine_nodes)

    def chain_step(initial, inputs):
        coarse_first, coarse_last, correction = inputs
        coarse_start = evaluate(initial, aggregate(initial))
        final_state = initial + step_length * (coarse_start + 0.5 * (coarse_last - coarse_first)) + correction
        return (final_state, (initial, coarse_start, final_state))
    unused, (initials, coarse_starts, finals) = lax.scan(chain_step, start_state, (coarse_firsts, coarse_lasts, corrections))

    def second_pass(inputs):
        fine_slice, coarse_first, coarse_last, initial, coarse_start, final_state = inputs
        coarse_end = evaluate(final_state, aggregate(final_state))
        change_first = coarse_start - coarse_first
        change_last = coarse_end - coarse_last
        fixed_first = fine_slice[0] + change_first
        fixed_middle = fine_slice[1] + 0.5 * (change_first + change_last)
        fixed_last = fine_slice[2] + change_last
        sweep_first = initial
        slope_first = evaluate(sweep_first, sweep_first)
        sweep_middle = sweep_first + 0.5 * step_length * (slope_first - fixed_first) + step_length * (5.0 * fixed_first + 8.0 * fixed_middle - fixed_last) / 24.0
        slope_middle = evaluate(sweep_middle, sweep_middle)
        sweep_last = sweep_middle + 0.5 * step_length * (slope_middle - fixed_middle) + step_length * (-fixed_first + 8.0 * fixed_middle + 5.0 * fixed_last) / 24.0
        return jnp.stack([sweep_first, sweep_middle, sweep_last])
    new_nodes = lax.map(second_pass, (fine_values, coarse_firsts, coarse_lasts, initials, coarse_starts, finals))
    next_start = jnp.concatenate([start_state[None], new_nodes[:-1, 2]], axis=0)
    return (new_nodes[:, :, 0:3], new_nodes[:, :, 3:6], next_start[:, 0:3], next_start[:, 3:6])
```

```python
import functools
import math

import jax
import jax.numpy as jnp
from jax import lax
from jax.experimental import pallas as pl
from jax.experimental.pallas import tpu as pltpu
from jax.sharding import PartitionSpec as P

CLUSTER = 16

core_squared = 0.01
step_length = 0.02


def rounded(value):
    return value.astype(jnp.bfloat16).astype(jnp.float32)


def split_three(value):
    one = rounded(value)
    two = rounded(value - one)
    return one, two, rounded(value - one - two)


def split_two(value):
    high = value.astype(jnp.bfloat16)
    return high, (value - high.astype(jnp.float32)).astype(jnp.bfloat16)


def product(left, right):
    return jnp.dot(left, right, preferred_element_type=jnp.float32)


def pad_rows(value):
    return jnp.concatenate([value, jnp.zeros((8 - value.shape[0], value.shape[1]), value.dtype)], axis=0)


def place_parts(state, extra):
    high = rounded(state[0:3])
    low = rounded(state[0:3] - high)
    used = high + low
    norm = used[0:1] * used[0:1] + used[1:2] * used[1:2] + used[2:3] * used[2:3] + extra
    return high, low, split_three(norm)


def source_places(state):
    high, low, norm = place_parts(state, 0.0)
    ones = jnp.ones_like(norm[0])
    none = jnp.zeros_like(norm[0])
    return jnp.concatenate(
        [high, norm[0], norm[1], norm[2], ones, ones]
        + [low, ones, none, none, none, none]
        + [high, none, none, none, none, none]
        + [low, none, none, none, none, none],
        axis=0,
    ).astype(jnp.bfloat16)


def target_places(state):
    high, low, norm = place_parts(state, core_squared)
    high = -2.0 * high
    low = -2.0 * low
    ones = jnp.ones_like(norm[0])
    none = jnp.zeros_like(norm[0])
    return jnp.concatenate(
        [high, ones, ones, ones, norm[0], norm[1]]
        + [high, norm[2], none, none, none, none]
        + [low, none, none, none, none, none]
        + [low, none, none, none, none, none],
        axis=0,
    ).astype(jnp.bfloat16)


def cross(left, right):
    return jnp.concatenate(
        [
            left[1:2] * right[2:3] - left[2:3] * right[1:2],
            left[2:3] * right[0:1] - left[0:1] * right[2:3],
            left[0:1] * right[1:2] - left[1:2] * right[0:1],
        ],
        axis=0,
    )


def source_moments(state):
    base = pad_rows(jnp.concatenate([state[3:6], cross(state[0:3], state[3:6])], axis=0))
    whole = jnp.concatenate([base, state[0:1] * base, state[1:2] * base, state[2:3] * base], axis=0)
    high = rounded(whole)
    low = whole - high
    for_q = jnp.concatenate([high[0:8], low[0:8]], axis=0).astype(jnp.bfloat16)
    for_h = jnp.concatenate([high, low], axis=0).astype(jnp.bfloat16)
    return for_q, for_h


def pair_sums(places, for_q, for_h, target):
    count = target.shape[1]
    sum_q = jnp.zeros((8, count), jnp.float32)
    sum_h = jnp.zeros((32, count), jnp.float32)
    length = places.shape[1]
    piece = math.gcd(length, 256)
    for begin in range(0, length, piece):
        part = slice(begin, begin + piece)
        spread = lax.dot_general(
            places[:, part], target, (((0,), (0,)), ((), ())), preferred_element_type=jnp.float32
        )
        inverse = lax.rsqrt(spread)
        square = inverse * inverse
        factor = square * inverse
        steep = factor * square
        factor_high, factor_low = split_two(factor)
        steep_high, steep_low = split_two(steep)
        got_q = product(for_q[:, part], factor_high) + product(for_q[:, part], factor_low)
        got_h = product(for_h[:, part], steep_high)
        low_h = product(for_h[0:32, part], steep_low)
        sum_q = sum_q + (got_q[0:8] + got_q[8:16])
        sum_h = sum_h + (got_h[0:32] + got_h[32:64] + low_h)
    return jnp.concatenate([sum_q, sum_h], axis=0)


def finish(sums, state, coupling):
    places = state[0:3]
    strengths = state[3:6]
    weighted = sums[0:3]
    velocity = cross(places, weighted) - sums[3:6]
    along = (
        strengths[0:1] * places[0:1] + strengths[1:2] * places[1:2] + strengths[2:3] * places[2:3]
    )
    moment = 3.0 * (
        along * sums[8:16]
        - strengths[0:1] * sums[16:24]
        - strengths[1:2] * sums[24:32]
        - strengths[2:3] * sums[32:40]
    )
    stretch = cross(strengths, weighted) - (cross(places, moment[0:3]) - moment[3:6])
    return -coupling * jnp.concatenate([velocity, stretch], axis=0)


def kernel(
    n_t,
    n_s,
    start_ref,
    nodes_ref,
    places_out,
    strengths_out,
    next_places_out,
    next_strengths_out,
    gathered,
    sums,
    steps,
    history,
    coarse,
    middles,
    handed,
    pool,
    send_a,
    recv_a,
    send_b,
    recv_b,
    send_d,
    recv_d,
    send_e,
    recv_e,
    send_w,
    recv_w,
    send_h,
    recv_h,
):
    length = start_ref.shape[1]
    coupling = 1.0 / (4.0 * math.pi * math.sqrt(length * n_s))
    mine = lax.axis_index("tm")
    me = lax.axis_index("space")

    def space_copy(source, target, send, recv, peer):
        return pltpu.make_async_remote_copy(
            src_ref=source, dst_ref=target, send_sem=send, recv_sem=recv,
            device_id={"space": peer}, device_id_type=pl.DeviceIdType.MESH,
        )

    def time_copy(source, target, send, recv, peer):
        return pltpu.make_async_remote_copy(
            src_ref=source, dst_ref=target, send_sem=send, recv_sem=recv,
            device_id={"tm": peer}, device_id_type=pl.DeviceIdType.MESH,
        )

    barrier = pltpu.get_barrier_semaphore()
    for offset in range(1, n_s):
        pl.semaphore_signal(
            barrier, inc=1, device_id={"space": lax.rem(me + offset, n_s)},
            device_id_type=pl.DeviceIdType.MESH,
        )
    for offset in range(1, n_t):
        pl.semaphore_signal(
            barrier, inc=1, device_id={"tm": lax.rem(mine + offset, n_t)},
            device_id_type=pl.DeviceIdType.MESH,
        )
    pl.semaphore_wait(barrier, n_s - 1 + n_t - 1)

    def node_copy(offset, slot):
        return space_copy(
            nodes_ref.at[0], gathered.at[slot], send_a.at[offset], recv_a.at[offset],
            lax.rem(me + offset, n_s),
        )

    def start_copy(offset, slot):
        return space_copy(
            start_ref, history.at[0, slot], send_b.at[offset], recv_b.at[offset],
            lax.rem(me + offset, n_s),
        )

    for offset in range(1, n_s):
        node_copy(offset, me).start()
    for offset in range(1, n_s):
        start_copy(offset, me).start()
    gathered[me] = nodes_ref[0]
    history[0, me] = start_ref[...]

    total = n_s * length
    clusters = total // CLUSTER
    particle = lax.broadcasted_iota(jnp.int32, (total, clusters), 0)
    cluster = lax.broadcasted_iota(jnp.int32, (total, clusters), 1)
    offset_in = particle - cluster * CLUSTER
    pool[...] = jnp.where((offset_in >= 0) & (offset_in < CLUSTER), 1.0, 0.0).astype(jnp.bfloat16)

    def aggregate(blocks):
        state = pad_rows(jnp.concatenate(blocks, axis=1))
        parts = jnp.concatenate(split_three(state), axis=0).astype(jnp.bfloat16)
        got = jnp.dot(parts, pool[...], preferred_element_type=jnp.float32)
        whole = got[0:8] + got[8:16] + got[16:24]
        return jnp.concatenate([whole[0:3] * (1.0 / CLUSTER), whole[3:6]], axis=0)

    def coarse_sources(blocks):
        merged = aggregate(blocks)
        return (source_places(merged),) + source_moments(merged)

    def fine_sums(source, target):
        for_q, for_h = source_moments(source)
        return pair_sums(source_places(source), for_q, for_h, target_places(target))

    for offset in range(n_s):
        source = lax.rem(me + n_s - offset, n_s)
        if offset > 0:
            node_copy(offset, source).wait_recv()

        def one_node(node, carry):
            got = fine_sums(gathered[source, node], nodes_ref[0, node])
            if offset == 0:
                sums[node] = got
            else:
                sums[node] = sums[node] + got
            return carry

        lax.fori_loop(0, 3, one_node, 0)

    fine = [finish(sums[node], nodes_ref[0, node], coupling) for node in range(3)]

    def coarse_value(blocks, target):
        return finish(pair_sums(*coarse_sources(blocks), target_places(target)), target, coupling)

    coarse_first = coarse_value([gathered[z, 0] for z in range(n_s)], nodes_ref[0, 0])
    coarse_last = coarse_value([gathered[z, 2] for z in range(n_s)], nodes_ref[0, 2])
    correction = step_length * (
        (fine[0] + 4.0 * fine[1] + fine[2]) / 6.0 - 0.5 * (coarse_first + coarse_last)
    )
    steps[mine, me] = correction + step_length * 0.5 * (coarse_last - coarse_first)

    def step_copy(offset, slot):
        return space_copy(
            steps.at[mine, me], steps.at[mine, slot], send_d.at[offset], recv_d.at[offset],
            lax.rem(me + offset, n_s),
        )

    for offset in range(1, n_s):
        step_copy(offset, me).start()
    for offset in range(1, n_s):
        start_copy(offset, lax.rem(me + n_s - offset, n_s)).wait_recv()
    for offset in range(1, n_s):
        step_copy(offset, lax.rem(me + n_s - offset, n_s)).wait_recv()

    def slice_copy(offset, slot):
        return time_copy(
            steps.at[slot], steps.at[slot], send_e.at[offset], recv_e.at[offset],
            lax.rem(mine + offset, n_t),
        )

    for offset in range(1, n_t):
        slice_copy(offset, mine).start()

    def chain_step(step, carry):
        sources = coarse_sources([history[step, z] for z in range(n_s)])

        @pl.when(step != mine)
        def _():
            slice_copy(lax.rem(mine + n_t - step, n_t), step).wait_recv()

        def one_block(z, inner):
            state = history[step, z]
            value = finish(pair_sums(*sources, target_places(state)), state, coupling)
            coarse[step, z] = value
            history[step + 1, z] = state + step_length * value + steps[step, z]
            return inner

        lax.fori_loop(0, n_s, one_block, 0, unroll=math.gcd(n_s, 4))
        return carry

    lax.fori_loop(0, n_t, chain_step, 0)

    initial = history[mine, me]
    final_state = history[mine + 1, me]
    coarse_end = coarse_value([history[mine + 1, z] for z in range(n_s)], final_state)
    change_first = coarse[mine, me] - coarse_first
    change_last = coarse_end - coarse_last
    fixed_first = fine[0] + change_first
    fixed_middle = fine[1] + 0.5 * (change_first + change_last)
    fixed_last = fine[2] + change_last

    sums[0] = jnp.zeros(sums.shape[1:], jnp.float32)

    def initial_block(z, carry):
        sums[0] = sums[0] + fine_sums(history[mine, z], history[mine, me])
        return carry

    lax.fori_loop(0, n_s, initial_block, 0)
    slope_first = finish(sums[0], initial, coupling)
    sweep_middle = (
        initial
        + 0.5 * step_length * (slope_first - fixed_first)
        + step_length * (5.0 * fixed_first + 8.0 * fixed_middle - fixed_last) / 24.0
    )
    middles[me] = sweep_middle

    def middle_copy(offset, slot):
        return space_copy(
            middles.at[me], middles.at[slot], send_w.at[offset], recv_w.at[offset],
            lax.rem(me + offset, n_s),
        )

    for offset in range(1, n_s):
        middle_copy(offset, me).start()
    places_out[0, 0] = initial[0:3]
    strengths_out[0, 0] = initial[3:6]
    places_out[0, 1] = sweep_middle[0:3]
    strengths_out[0, 1] = sweep_middle[3:6]
    sums[1] = fine_sums(sweep_middle, sweep_middle)
    for offset in range(1, n_s):
        source = lax.rem(me + n_s - offset, n_s)
        middle_copy(offset, source).wait_recv()
        sums[1] = sums[1] + fine_sums(middles[source], sweep_middle)
    slope_middle = finish(sums[1], sweep_middle, coupling)
    sweep_last = (
        sweep_middle
        + 0.5 * step_length * (slope_middle - fixed_middle)
        + step_length * (-fixed_first + 8.0 * fixed_middle + 5.0 * fixed_last) / 24.0
    )
    handed[0] = sweep_last

    def last_copy():
        return time_copy(handed.at[0], handed.at[1], send_h, recv_h, lax.rem(mine + 1, n_t))

    @pl.when(mine < n_t - 1)
    def _():
        last_copy().start()

    places_out[0, 2] = sweep_last[0:3]
    strengths_out[0, 2] = sweep_last[3:6]
    for offset in range(1, n_s):
        node_copy(offset, me).wait_send()
        start_copy(offset, me).wait_send()
        step_copy(offset, me).wait_send()
        middle_copy(offset, me).wait_send()
    for offset in range(1, n_t):
        slice_copy(offset, mine).wait_send()

    @pl.when(mine == 0)
    def _():
        next_places_out[0] = start_ref[0:3]
        next_strengths_out[0] = start_ref[3:6]

    @pl.when(mine > 0)
    def _():
        last_copy().wait_recv()
        next_places_out[0] = handed[1, 0:3]
        next_strengths_out[0] = handed[1, 3:6]

    @pl.when(mine < n_t - 1)
    def _():
        last_copy().wait_send()


def solution(mesh):
    n_t, n_s = mesh.shape["tm"], mesh.shape["space"]

    def shards(start_state, fine_nodes):
        length = start_state.shape[1]
        total = length * n_s
        vmem = pl.BlockSpec(memory_space=pltpu.VMEM)
        dma = pltpu.SemaphoreType.DMA
        return pl.pallas_call(
            functools.partial(kernel, n_t, n_s),
            out_shape=(
                jax.ShapeDtypeStruct((1, 3, 3, length), jnp.float32),
                jax.ShapeDtypeStruct((1, 3, 3, length), jnp.float32),
                jax.ShapeDtypeStruct((1, 3, length), jnp.float32),
                jax.ShapeDtypeStruct((1, 3, length), jnp.float32),
            ),
            in_specs=[vmem, vmem],
            out_specs=(vmem, vmem, vmem, vmem),
            scratch_shapes=[
                pltpu.VMEM((n_s, 3, 6, length), jnp.float32),
                pltpu.VMEM((3, 40, length), jnp.float32),
                pltpu.VMEM((n_t, n_s, 6, length), jnp.float32),
                pltpu.VMEM((n_t + 1, n_s, 6, length), jnp.float32),
                pltpu.VMEM((n_t, n_s, 6, length), jnp.float32),
                pltpu.VMEM((n_s, 6, length), jnp.float32),
                pltpu.VMEM((2, 6, length), jnp.float32),
                pltpu.VMEM((total, total // CLUSTER), jnp.bfloat16),
                dma((n_s,)), dma((n_s,)),
                dma((n_s,)), dma((n_s,)),
                dma((n_s,)), dma((n_s,)),
                dma((n_t,)), dma((n_t,)),
                dma((n_s,)), dma((n_s,)),
                dma, dma,
            ],
            compiler_params=pltpu.CompilerParams(collective_id=0, has_side_effects=True),
        )(start_state, fine_nodes)

    return jax.shard_map(
        shards,
        mesh=mesh,
        in_specs=(P(None, "space"), P("tm", None, None, "space")),
        out_specs=(
            P("tm", None, None, "space"),
            P("tm", None, None, "space"),
            P("tm", None, "space"),
            P("tm", None, "space"),
        ),
        check_vma=False,
    )
```

```python
import functools
import math

import jax
import jax.numpy as jnp
from jax import lax
from jax.experimental import pallas as pl
from jax.experimental.pallas import tpu as pltpu
from jax.sharding import PartitionSpec as P

CLUSTER = 16

core_squared = 0.01
step_length = 0.02


def rounded(value):
    return value.astype(jnp.bfloat16).astype(jnp.float32)


def split_three(value):
    one = rounded(value)
    two = rounded(value - one)
    return one, two, rounded(value - one - two)


def split_two(value):
    high = value.astype(jnp.bfloat16)
    return high, (value - high.astype(jnp.float32)).astype(jnp.bfloat16)


def product(left, right):
    return jnp.dot(left, right, preferred_element_type=jnp.float32)


def pad_rows(value):
    return jnp.concatenate([value, jnp.zeros((8 - value.shape[0], value.shape[1]), value.dtype)], axis=0)


def place_parts(state, extra):
    high = rounded(state[0:3])
    low = rounded(state[0:3] - high)
    used = high + low
    norm = used[0:1] * used[0:1] + used[1:2] * used[1:2] + used[2:3] * used[2:3] + extra
    return high, low, split_three(norm)


def source_places(state):
    high, low, norm = place_parts(state, 0.0)
    ones = jnp.ones_like(norm[0])
    none = jnp.zeros_like(norm[0])
    return jnp.concatenate(
        [high, norm[0], norm[1], norm[2], ones, ones]
        + [low, ones, none, none, none, none]
        + [high, none, none, none, none, none]
        + [low, none, none, none, none, none],
        axis=0,
    ).astype(jnp.bfloat16)


def target_places(state):
    high, low, norm = place_parts(state, core_squared)
    high = -2.0 * high
    low = -2.0 * low
    ones = jnp.ones_like(norm[0])
    none = jnp.zeros_like(norm[0])
    return jnp.concatenate(
        [high, ones, ones, ones, norm[0], norm[1]]
        + [high, norm[2], none, none, none, none]
        + [low, none, none, none, none, none]
        + [low, none, none, none, none, none],
        axis=0,
    ).astype(jnp.bfloat16)


def cross(left, right):
    return jnp.concatenate(
        [
            left[1:2] * right[2:3] - left[2:3] * right[1:2],
            left[2:3] * right[0:1] - left[0:1] * right[2:3],
            left[0:1] * right[1:2] - left[1:2] * right[0:1],
        ],
        axis=0,
    )


def source_moments(state):
    base = pad_rows(jnp.concatenate([state[3:6], cross(state[0:3], state[3:6])], axis=0))
    whole = jnp.concatenate([base, state[0:1] * base, state[1:2] * base, state[2:3] * base], axis=0)
    parts = split_three(whole)
    for_q = jnp.concatenate([part[0:8] for part in parts] + [jnp.zeros_like(base)], axis=0)
    for_q = for_q.astype(jnp.bfloat16)
    for_h = jnp.concatenate(parts, axis=0).astype(jnp.bfloat16)
    return for_q, for_h


def pair_sums(places, for_q, for_h, target):
    count = target.shape[1]
    sum_q = jnp.zeros((8, count), jnp.float32)
    sum_h = jnp.zeros((32, count), jnp.float32)
    length = places.shape[1]
    piece = math.gcd(length, 256)
    for begin in range(0, length, piece):
        part = slice(begin, begin + piece)
        spread = lax.dot_general(
            places[:, part], target, (((0,), (0,)), ((), ())), preferred_element_type=jnp.float32
        )
        inverse = lax.rsqrt(spread)
        square = inverse * inverse
        factor = square * inverse
        steep = factor * square
        factor_high, factor_low = split_two(factor)
        steep_high, steep_low = split_two(steep)
        got_q = product(for_q[:, part], factor_high)
        low_q = product(for_q[0:16, part], factor_low)
        got_h = product(for_h[:, part], steep_high)
        low_h = product(for_h[0:32, part], steep_low)
        sum_q = sum_q + (got_q[0:8] + (got_q[8:16] + (got_q[16:24] + low_q[0:8])))
        sum_h = sum_h + (got_h[0:32] + (got_h[32:64] + (got_h[64:96] + low_h)))
    return jnp.concatenate([sum_q, sum_h], axis=0)


def finish(sums, state, coupling):
    places = state[0:3]
    strengths = state[3:6]
    weighted = sums[0:3]
    velocity = cross(places, weighted) - sums[3:6]
    along = (
        strengths[0:1] * places[0:1] + strengths[1:2] * places[1:2] + strengths[2:3] * places[2:3]
    )
    moment = 3.0 * (
        along * sums[8:16]
        - strengths[0:1] * sums[16:24]
        - strengths[1:2] * sums[24:32]
        - strengths[2:3] * sums[32:40]
    )
    stretch = cross(strengths, weighted) - (cross(places, moment[0:3]) - moment[3:6])
    return -coupling * jnp.concatenate([velocity, stretch], axis=0)


def kernel(
    n_t,
    n_s,
    start_ref,
    nodes_ref,
    places_out,
    strengths_out,
    next_places_out,
    next_strengths_out,
    gathered,
    sums,
    steps,
    history,
    coarse,
    middles,
    handed,
    pool,
    send_a,
    recv_a,
    send_b,
    recv_b,
    send_d,
    recv_d,
    send_e,
    recv_e,
    send_w,
    recv_w,
    send_h,
    recv_h,
):
    length = start_ref.shape[1]
    coupling = 1.0 / (4.0 * math.pi * math.sqrt(length * n_s))
    mine = lax.axis_index("tm")
    me = lax.axis_index("space")

    def space_copy(source, target, send, recv, peer):
        return pltpu.make_async_remote_copy(
            src_ref=source, dst_ref=target, send_sem=send, recv_sem=recv,
            device_id={"space": peer}, device_id_type=pl.DeviceIdType.MESH,
        )

    def time_copy(source, target, send, recv, peer):
        return pltpu.make_async_remote_copy(
            src_ref=source, dst_ref=target, send_sem=send, recv_sem=recv,
            device_id={"tm": peer}, device_id_type=pl.DeviceIdType.MESH,
        )

    lanes = nodes_ref.shape[1]
    pieces = length // lanes

    def put(target, row, value):
        for one in range(value.shape[0]):
            for piece in range(pieces):
                target[row + one, piece : piece + 1, :] = value[
                    one : one + 1, piece * lanes : (piece + 1) * lanes
                ]

    barrier = pltpu.get_barrier_semaphore()
    for offset in range(1, n_s):
        pl.semaphore_signal(
            barrier, inc=1, device_id={"space": lax.rem(me + offset, n_s)},
            device_id_type=pl.DeviceIdType.MESH,
        )
    for offset in range(1, n_t):
        pl.semaphore_signal(
            barrier, inc=1, device_id={"tm": lax.rem(mine + offset, n_t)},
            device_id_type=pl.DeviceIdType.MESH,
        )
    for node in range(3):
        for row in range(6):
            for piece in range(pieces):
                at = (node * 6 + row) * pieces + piece
                gathered[me, node, row : row + 1, piece * lanes : (piece + 1) * lanes] = nodes_ref[
                    at : at + 1, :
                ]
    pl.semaphore_wait(barrier, n_s - 1 + n_t - 1)

    def node_copy(offset, slot):
        return space_copy(
            gathered.at[me], gathered.at[slot], send_a.at[offset], recv_a.at[offset],
            lax.rem(me + offset, n_s),
        )

    def start_copy(offset, slot):
        return space_copy(
            start_ref, history.at[0, slot], send_b.at[offset], recv_b.at[offset],
            lax.rem(me + offset, n_s),
        )

    for offset in range(1, n_s):
        node_copy(offset, me).start()
    for offset in range(1, n_s):
        start_copy(offset, me).start()
    history[0, me] = start_ref[...]

    total = n_s * length
    clusters = total // CLUSTER
    particle = lax.broadcasted_iota(jnp.int32, (total, clusters), 0)
    cluster = lax.broadcasted_iota(jnp.int32, (total, clusters), 1)
    offset_in = particle - cluster * CLUSTER
    pool[...] = jnp.where((offset_in >= 0) & (offset_in < CLUSTER), 1.0, 0.0).astype(jnp.bfloat16)

    def aggregate(blocks):
        state = pad_rows(jnp.concatenate(blocks, axis=1))
        parts = jnp.concatenate(split_three(state), axis=0).astype(jnp.bfloat16)
        got = jnp.dot(parts, pool[...], preferred_element_type=jnp.float32)
        whole = got[0:8] + got[8:16] + got[16:24]
        return jnp.concatenate([whole[0:3] * (1.0 / CLUSTER), whole[3:6]], axis=0)

    def coarse_sources(blocks):
        merged = aggregate(blocks)
        return (source_places(merged),) + source_moments(merged)

    def fine_sums(source, target):
        for_q, for_h = source_moments(source)
        return pair_sums(source_places(source), for_q, for_h, target_places(target))

    for offset in range(n_s):
        source = lax.rem(me + n_s - offset, n_s)
        if offset > 0:
            node_copy(offset, source).wait_recv()

        def one_node(node, carry):
            got = fine_sums(gathered[source, node], gathered[me, node])
            if offset == 0:
                sums[node] = got
            else:
                sums[node] = sums[node] + got
            return carry

        lax.fori_loop(0, 3, one_node, 0)

    fine = [finish(sums[node], gathered[me, node], coupling) for node in range(3)]

    def coarse_value(blocks, target):
        return finish(pair_sums(*coarse_sources(blocks), target_places(target)), target, coupling)

    coarse_first = coarse_value([gathered[z, 0] for z in range(n_s)], gathered[me, 0])
    coarse_last = coarse_value([gathered[z, 2] for z in range(n_s)], gathered[me, 2])
    correction = step_length * (
        (fine[0] + 4.0 * fine[1] + fine[2]) / 6.0 - 0.5 * (coarse_first + coarse_last)
    )
    steps[mine, me] = correction + step_length * 0.5 * (coarse_last - coarse_first)

    def step_copy(offset, slot):
        return space_copy(
            steps.at[mine, me], steps.at[mine, slot], send_d.at[offset], recv_d.at[offset],
            lax.rem(me + offset, n_s),
        )

    for offset in range(1, n_s):
        step_copy(offset, me).start()
    for offset in range(1, n_s):
        start_copy(offset, lax.rem(me + n_s - offset, n_s)).wait_recv()
    for offset in range(1, n_s):
        step_copy(offset, lax.rem(me + n_s - offset, n_s)).wait_recv()

    def slice_copy(offset, slot):
        return time_copy(
            steps.at[slot], steps.at[slot], send_e.at[offset], recv_e.at[offset],
            lax.rem(mine + offset, n_t),
        )

    for offset in range(1, n_t):
        slice_copy(offset, mine).start()

    def chain_step(step, carry):
        sources = coarse_sources([history[step, z] for z in range(n_s)])

        @pl.when(step != mine)
        def _():
            slice_copy(lax.rem(mine + n_t - step, n_t), step).wait_recv()

        def one_block(z, inner):
            state = history[step, z]
            value = finish(pair_sums(*sources, target_places(state)), state, coupling)
            coarse[step, z] = value
            history[step + 1, z] = state + step_length * value + steps[step, z]
            return inner

        lax.fori_loop(0, n_s, one_block, 0, unroll=math.gcd(n_s, 4))
        return carry

    lax.fori_loop(0, n_t, chain_step, 0)

    initial = history[mine, me]
    final_state = history[mine + 1, me]
    coarse_end = coarse_value([history[mine + 1, z] for z in range(n_s)], final_state)
    change_first = coarse[mine, me] - coarse_first
    change_last = coarse_end - coarse_last
    fixed_first = fine[0] + change_first
    fixed_middle = fine[1] + 0.5 * (change_first + change_last)
    fixed_last = fine[2] + change_last

    sums[0] = jnp.zeros(sums.shape[1:], jnp.float32)

    def initial_block(z, carry):
        sums[0] = sums[0] + fine_sums(history[mine, z], history[mine, me])
        return carry

    lax.fori_loop(0, n_s, initial_block, 0)
    slope_first = finish(sums[0], initial, coupling)
    sweep_middle = (
        initial
        + 0.5 * step_length * (slope_first - fixed_first)
        + step_length * (5.0 * fixed_first + 8.0 * fixed_middle - fixed_last) / 24.0
    )
    middles[me] = sweep_middle

    def middle_copy(offset, slot):
        return space_copy(
            middles.at[me], middles.at[slot], send_w.at[offset], recv_w.at[offset],
            lax.rem(me + offset, n_s),
        )

    for offset in range(1, n_s):
        middle_copy(offset, me).start()
    put(places_out, 0, initial[0:3])
    put(strengths_out, 0, initial[3:6])
    put(places_out, 3, sweep_middle[0:3])
    put(strengths_out, 3, sweep_middle[3:6])
    sums[1] = fine_sums(sweep_middle, sweep_middle)
    for offset in range(1, n_s):
        source = lax.rem(me + n_s - offset, n_s)
        middle_copy(offset, source).wait_recv()
        sums[1] = sums[1] + fine_sums(middles[source], sweep_middle)
    slope_middle = finish(sums[1], sweep_middle, coupling)
    sweep_last = (
        sweep_middle
        + 0.5 * step_length * (slope_middle - fixed_middle)
        + step_length * (-fixed_first + 8.0 * fixed_middle + 5.0 * fixed_last) / 24.0
    )
    put(handed.at[0], 0, sweep_last)

    def last_copy():
        return time_copy(handed.at[0], handed.at[1], send_h, recv_h, lax.rem(mine + 1, n_t))

    @pl.when(mine < n_t - 1)
    def _():
        last_copy().start()

    places_out[6:9] = handed[0, 0:3]
    strengths_out[6:9] = handed[0, 3:6]
    for offset in range(1, n_s):
        node_copy(offset, me).wait_send()
        start_copy(offset, me).wait_send()
        step_copy(offset, me).wait_send()
        middle_copy(offset, me).wait_send()
    for offset in range(1, n_t):
        slice_copy(offset, mine).wait_send()

    @pl.when(mine == 0)
    def _():
        put(next_places_out, 0, start_ref[0:3])
        put(next_strengths_out, 0, start_ref[3:6])

    @pl.when(mine > 0)
    def _():
        last_copy().wait_recv()
        next_places_out[...] = handed[1, 0:3]
        next_strengths_out[...] = handed[1, 3:6]

    @pl.when(mine < n_t - 1)
    def _():
        last_copy().wait_send()


def solution(mesh):
    n_t, n_s = mesh.shape["tm"], mesh.shape["space"]

    def shards(start_state, fine_nodes):
        length = start_state.shape[1]
        total = length * n_s
        vmem = pl.BlockSpec(memory_space=pltpu.VMEM)
        dma = pltpu.SemaphoreType.DMA
        lanes = math.gcd(length, 128)
        rows = (length // lanes, lanes)
        results = pl.pallas_call(
            functools.partial(kernel, n_t, n_s),
            out_shape=(
                jax.ShapeDtypeStruct((9,) + rows, jnp.float32),
                jax.ShapeDtypeStruct((9,) + rows, jnp.float32),
                jax.ShapeDtypeStruct((3,) + rows, jnp.float32),
                jax.ShapeDtypeStruct((3,) + rows, jnp.float32),
            ),
            in_specs=[vmem, vmem],
            out_specs=(vmem, vmem, vmem, vmem),
            scratch_shapes=[
                pltpu.VMEM((n_s, 3, 6, length), jnp.float32),
                pltpu.VMEM((3, 40, length), jnp.float32),
                pltpu.VMEM((n_t, n_s, 6, length), jnp.float32),
                pltpu.VMEM((n_t + 1, n_s, 6, length), jnp.float32),
                pltpu.VMEM((n_t, n_s, 6, length), jnp.float32),
                pltpu.VMEM((n_s, 6, length), jnp.float32),
                pltpu.VMEM((2, 6) + rows, jnp.float32),
                pltpu.VMEM((total, total // CLUSTER), jnp.bfloat16),
                dma((n_s,)), dma((n_s,)),
                dma((n_s,)), dma((n_s,)),
                dma((n_s,)), dma((n_s,)),
                dma((n_t,)), dma((n_t,)),
                dma((n_s,)), dma((n_s,)),
                dma, dma,
            ],
            compiler_params=pltpu.CompilerParams(collective_id=0, has_side_effects=True),
        )(start_state, fine_nodes.reshape(-1, lanes))
        nodes, ends = (1, 3, 3, length), (1, 3, length)
        return tuple(
            one.reshape(shape) for one, shape in zip(results, (nodes, nodes, ends, ends))
        )

    return jax.shard_map(
        shards,
        mesh=mesh,
        in_specs=(P(None, "space"), P("tm", None, None, "space")),
        out_specs=(
            P("tm", None, None, "space"),
            P("tm", None, None, "space"),
            P("tm", None, "space"),
            P("tm", None, "space"),
        ),
        check_vma=False,
    )
```

```python
import functools
import math

import jax
import jax.numpy as jnp
from jax import lax
from jax.experimental import pallas as pl
from jax.experimental.pallas import tpu as pltpu
from jax.sharding import PartitionSpec as P

CLUSTER = 16

core_squared = 0.01
step_length = 0.02


def rounded(value):
    return value.astype(jnp.bfloat16).astype(jnp.float32)


def split_three(value):
    one = rounded(value)
    two = rounded(value - one)
    return one, two, rounded(value - one - two)


def split_two(value):
    high = value.astype(jnp.bfloat16)
    return high, (value - high.astype(jnp.float32)).astype(jnp.bfloat16)


def product(left, right):
    return jnp.dot(left, right, preferred_element_type=jnp.float32)


def pad_rows(value):
    return jnp.concatenate([value, jnp.zeros((8 - value.shape[0], value.shape[1]), value.dtype)], axis=0)


def place_parts(state, extra):
    high = rounded(state[0:3])
    low = rounded(state[0:3] - high)
    used = high + low
    norm = used[0:1] * used[0:1] + used[1:2] * used[1:2] + used[2:3] * used[2:3] + extra
    return high, low, split_three(norm)


def source_places(state):
    high, low, norm = place_parts(state, 0.0)
    ones = jnp.ones_like(norm[0])
    none = jnp.zeros_like(norm[0])
    return jnp.concatenate(
        [high, norm[0], norm[1], norm[2], ones, ones]
        + [low, ones, none, none, none, none]
        + [high, none, none, none, none, none]
        + [low, none, none, none, none, none],
        axis=0,
    ).astype(jnp.bfloat16)


def target_places(state):
    high, low, norm = place_parts(state, core_squared)
    high = -2.0 * high
    low = -2.0 * low
    ones = jnp.ones_like(norm[0])
    none = jnp.zeros_like(norm[0])
    return jnp.concatenate(
        [high, ones, ones, ones, norm[0], norm[1]]
        + [high, norm[2], none, none, none, none]
        + [low, none, none, none, none, none]
        + [low, none, none, none, none, none],
        axis=0,
    ).astype(jnp.bfloat16)


def cross(left, right):
    return jnp.concatenate(
        [
            left[1:2] * right[2:3] - left[2:3] * right[1:2],
            left[2:3] * right[0:1] - left[0:1] * right[2:3],
            left[0:1] * right[1:2] - left[1:2] * right[0:1],
        ],
        axis=0,
    )


def source_moments(state):
    base = pad_rows(jnp.concatenate([state[3:6], cross(state[0:3], state[3:6])], axis=0))
    whole = jnp.concatenate([base, state[0:1] * base, state[1:2] * base, state[2:3] * base], axis=0)
    parts = split_three(whole)
    for_q = jnp.concatenate([part[0:8] for part in parts] + [jnp.zeros_like(base)], axis=0)
    for_q = for_q.astype(jnp.bfloat16)
    for_h = jnp.concatenate(parts, axis=0).astype(jnp.bfloat16)
    return for_q, for_h


def pair_sums(places, for_q, for_h, target, both=True):
    count = target.shape[1]
    sum_q = jnp.zeros((8, count), jnp.float32)
    sum_h = jnp.zeros((32, count), jnp.float32)
    length = places.shape[1]
    piece = math.gcd(length, 256)
    for begin in range(0, length, piece):
        part = slice(begin, begin + piece)
        spread = lax.dot_general(
            places[:, part], target, (((0,), (0,)), ((), ())), preferred_element_type=jnp.float32
        )
        inverse = lax.rsqrt(spread)
        square = inverse * inverse
        factor = square * inverse
        steep = factor * square
        factor_high, factor_low = split_two(factor)
        steep_high, steep_low = split_two(steep)
        got_q = product(for_q[:, part], factor_high)
        got_h = product(for_h[:, part], steep_high)
        rest_q = got_q[8:16] + got_q[16:24]
        rest_h = got_h[32:64] + got_h[64:96]
        if both:
            rest_q = rest_q + product(for_q[0:16, part], factor_low)[0:8]
            rest_h = rest_h + product(for_h[0:32, part], steep_low)
        sum_q = sum_q + (got_q[0:8] + rest_q)
        sum_h = sum_h + (got_h[0:32] + rest_h)
    return jnp.concatenate([sum_q, sum_h], axis=0)


def finish(sums, state, coupling):
    places = state[0:3]
    strengths = state[3:6]
    weighted = sums[0:3]
    velocity = cross(places, weighted) - sums[3:6]
    along = (
        strengths[0:1] * places[0:1] + strengths[1:2] * places[1:2] + strengths[2:3] * places[2:3]
    )
    moment = 3.0 * (
        along * sums[8:16]
        - strengths[0:1] * sums[16:24]
        - strengths[1:2] * sums[24:32]
        - strengths[2:3] * sums[32:40]
    )
    stretch = cross(strengths, weighted) - (cross(places, moment[0:3]) - moment[3:6])
    return -coupling * jnp.concatenate([velocity, stretch], axis=0)


def kernel(
    n_t,
    n_s,
    start_ref,
    nodes_ref,
    places_out,
    strengths_out,
    next_places_out,
    next_strengths_out,
    gathered,
    sums,
    steps,
    history,
    coarse,
    middles,
    handed,
    pool,
    send_a,
    recv_a,
    send_b,
    recv_b,
    send_d,
    recv_d,
    send_e,
    recv_e,
    send_w,
    recv_w,
    send_h,
    recv_h,
):
    length = start_ref.shape[1]
    coupling = 1.0 / (4.0 * math.pi * math.sqrt(length * n_s))
    mine = lax.axis_index("tm")
    me = lax.axis_index("space")

    def space_copy(source, target, send, recv, peer):
        return pltpu.make_async_remote_copy(
            src_ref=source, dst_ref=target, send_sem=send, recv_sem=recv,
            device_id={"space": peer}, device_id_type=pl.DeviceIdType.MESH,
        )

    def time_copy(source, target, send, recv, peer):
        return pltpu.make_async_remote_copy(
            src_ref=source, dst_ref=target, send_sem=send, recv_sem=recv,
            device_id={"tm": peer}, device_id_type=pl.DeviceIdType.MESH,
        )

    lanes = nodes_ref.shape[1]
    pieces = length // lanes

    def put(target, row, value):
        for one in range(value.shape[0]):
            for piece in range(pieces):
                target[row + one, piece : piece + 1, :] = value[
                    one : one + 1, piece * lanes : (piece + 1) * lanes
                ]

    barrier = pltpu.get_barrier_semaphore()
    for offset in range(1, n_s):
        pl.semaphore_signal(
            barrier, inc=1, device_id={"space": lax.rem(me + offset, n_s)},
            device_id_type=pl.DeviceIdType.MESH,
        )
    for offset in range(1, n_t):
        pl.semaphore_signal(
            barrier, inc=1, device_id={"tm": lax.rem(mine + offset, n_t)},
            device_id_type=pl.DeviceIdType.MESH,
        )
    for node in range(3):
        for row in range(6):
            for piece in range(pieces):
                at = (node * 6 + row) * pieces + piece
                gathered[me, node, row : row + 1, piece * lanes : (piece + 1) * lanes] = nodes_ref[
                    at : at + 1, :
                ]
    pl.semaphore_wait(barrier, n_s - 1 + n_t - 1)

    def node_copy(offset, slot):
        return space_copy(
            gathered.at[me], gathered.at[slot], send_a.at[offset], recv_a.at[offset],
            lax.rem(me + offset, n_s),
        )

    def start_copy(offset, slot):
        return space_copy(
            start_ref, history.at[0, slot], send_b.at[offset], recv_b.at[offset],
            lax.rem(me + offset, n_s),
        )

    for offset in range(1, n_s):
        node_copy(offset, me).start()
    for offset in range(1, n_s):
        start_copy(offset, me).start()
    history[0, me] = start_ref[...]

    total = n_s * length
    clusters = total // CLUSTER
    particle = lax.broadcasted_iota(jnp.int32, (total, clusters), 0)
    cluster = lax.broadcasted_iota(jnp.int32, (total, clusters), 1)
    offset_in = particle - cluster * CLUSTER
    pool[...] = jnp.where((offset_in >= 0) & (offset_in < CLUSTER), 1.0, 0.0).astype(jnp.bfloat16)

    def aggregate(blocks):
        state = pad_rows(jnp.concatenate(blocks, axis=1))
        parts = jnp.concatenate(split_three(state), axis=0).astype(jnp.bfloat16)
        got = jnp.dot(parts, pool[...], preferred_element_type=jnp.float32)
        whole = got[0:8] + got[8:16] + got[16:24]
        return jnp.concatenate([whole[0:3] * (1.0 / CLUSTER), whole[3:6]], axis=0)

    def coarse_sources(blocks):
        merged = aggregate(blocks)
        return (source_places(merged),) + source_moments(merged)

    def fine_sums(source, target, both=True):
        for_q, for_h = source_moments(source)
        return pair_sums(source_places(source), for_q, for_h, target_places(target), both)

    for offset in range(n_s):
        source = lax.rem(me + n_s - offset, n_s)
        if offset > 0:
            node_copy(offset, source).wait_recv()

        def one_node(node, carry):
            got = fine_sums(gathered[source, node], gathered[me, node])
            if offset == 0:
                sums[node] = got
            else:
                sums[node] = sums[node] + got
            return carry

        lax.fori_loop(0, 3, one_node, 0)

    fine = [finish(sums[node], gathered[me, node], coupling) for node in range(3)]

    def coarse_value(blocks, target):
        return finish(pair_sums(*coarse_sources(blocks), target_places(target)), target, coupling)

    coarse_first = coarse_value([gathered[z, 0] for z in range(n_s)], gathered[me, 0])
    coarse_last = coarse_value([gathered[z, 2] for z in range(n_s)], gathered[me, 2])
    correction = step_length * (
        (fine[0] + 4.0 * fine[1] + fine[2]) / 6.0 - 0.5 * (coarse_first + coarse_last)
    )
    steps[mine, me] = correction + step_length * 0.5 * (coarse_last - coarse_first)

    def step_copy(offset, slot):
        return space_copy(
            steps.at[mine, me], steps.at[mine, slot], send_d.at[offset], recv_d.at[offset],
            lax.rem(me + offset, n_s),
        )

    for offset in range(1, n_s):
        step_copy(offset, me).start()
    for offset in range(1, n_s):
        start_copy(offset, lax.rem(me + n_s - offset, n_s)).wait_recv()
    for offset in range(1, n_s):
        step_copy(offset, lax.rem(me + n_s - offset, n_s)).wait_recv()

    def slice_copy(offset, slot):
        return time_copy(
            steps.at[slot], steps.at[slot], send_e.at[offset], recv_e.at[offset],
            lax.rem(mine + offset, n_t),
        )

    for offset in range(1, n_t):
        slice_copy(offset, mine).start()

    def chain_step(step, carry):
        sources = coarse_sources([history[step, z] for z in range(n_s)])

        @pl.when(step != mine)
        def _():
            slice_copy(lax.rem(mine + n_t - step, n_t), step).wait_recv()

        def one_block(z, inner):
            state = history[step, z]
            value = finish(pair_sums(*sources, target_places(state)), state, coupling)
            coarse[step, z] = value
            history[step + 1, z] = state + step_length * value + steps[step, z]
            return inner

        lax.fori_loop(0, n_s, one_block, 0, unroll=math.gcd(n_s, 4))
        return carry

    lax.fori_loop(0, n_t, chain_step, 0)

    initial = history[mine, me]
    final_state = history[mine + 1, me]
    coarse_end = coarse_value([history[mine + 1, z] for z in range(n_s)], final_state)
    change_first = coarse[mine, me] - coarse_first
    change_last = coarse_end - coarse_last
    fixed_first = fine[0] + change_first
    fixed_middle = fine[1] + 0.5 * (change_first + change_last)
    fixed_last = fine[2] + change_last

    sums[0] = jnp.zeros(sums.shape[1:], jnp.float32)

    def initial_block(z, carry):
        sums[0] = sums[0] + fine_sums(history[mine, z], history[mine, me], False)
        return carry

    lax.fori_loop(0, n_s, initial_block, 0)
    slope_first = finish(sums[0], initial, coupling)
    sweep_middle = (
        initial
        + 0.5 * step_length * (slope_first - fixed_first)
        + step_length * (5.0 * fixed_first + 8.0 * fixed_middle - fixed_last) / 24.0
    )
    middles[me] = sweep_middle

    def middle_copy(offset, slot):
        return space_copy(
            middles.at[me], middles.at[slot], send_w.at[offset], recv_w.at[offset],
            lax.rem(me + offset, n_s),
        )

    for offset in range(1, n_s):
        middle_copy(offset, me).start()
    put(places_out, 0, initial[0:3])
    put(strengths_out, 0, initial[3:6])
    put(places_out, 3, sweep_middle[0:3])
    put(strengths_out, 3, sweep_middle[3:6])
    sums[1] = fine_sums(sweep_middle, sweep_middle, False)
    for offset in range(1, n_s):
        source = lax.rem(me + n_s - offset, n_s)
        middle_copy(offset, source).wait_recv()
        sums[1] = sums[1] + fine_sums(middles[source], sweep_middle, False)
    slope_middle = finish(sums[1], sweep_middle, coupling)
    sweep_last = (
        sweep_middle
        + 0.5 * step_length * (slope_middle - fixed_middle)
        + step_length * (-fixed_first + 8.0 * fixed_middle + 5.0 * fixed_last) / 24.0
    )
    put(handed.at[0], 0, sweep_last)

    def last_copy():
        return time_copy(handed.at[0], handed.at[1], send_h, recv_h, lax.rem(mine + 1, n_t))

    @pl.when(mine < n_t - 1)
    def _():
        last_copy().start()

    places_out[6:9] = handed[0, 0:3]
    strengths_out[6:9] = handed[0, 3:6]
    for offset in range(1, n_s):
        node_copy(offset, me).wait_send()
        start_copy(offset, me).wait_send()
        step_copy(offset, me).wait_send()
        middle_copy(offset, me).wait_send()
    for offset in range(1, n_t):
        slice_copy(offset, mine).wait_send()

    @pl.when(mine == 0)
    def _():
        put(next_places_out, 0, start_ref[0:3])
        put(next_strengths_out, 0, start_ref[3:6])

    @pl.when(mine > 0)
    def _():
        last_copy().wait_recv()
        next_places_out[...] = handed[1, 0:3]
        next_strengths_out[...] = handed[1, 3:6]

    @pl.when(mine < n_t - 1)
    def _():
        last_copy().wait_send()


def solution(mesh):
    n_t, n_s = mesh.shape["tm"], mesh.shape["space"]

    def shards(start_state, fine_nodes):
        length = start_state.shape[1]
        total = length * n_s
        vmem = pl.BlockSpec(memory_space=pltpu.VMEM)
        dma = pltpu.SemaphoreType.DMA
        lanes = math.gcd(length, 128)
        rows = (length // lanes, lanes)
        results = pl.pallas_call(
            functools.partial(kernel, n_t, n_s),
            out_shape=(
                jax.ShapeDtypeStruct((9,) + rows, jnp.float32),
                jax.ShapeDtypeStruct((9,) + rows, jnp.float32),
                jax.ShapeDtypeStruct((3,) + rows, jnp.float32),
                jax.ShapeDtypeStruct((3,) + rows, jnp.float32),
            ),
            in_specs=[vmem, vmem],
            out_specs=(vmem, vmem, vmem, vmem),
            scratch_shapes=[
                pltpu.VMEM((n_s, 3, 6, length), jnp.float32),
                pltpu.VMEM((3, 40, length), jnp.float32),
                pltpu.VMEM((n_t, n_s, 6, length), jnp.float32),
                pltpu.VMEM((n_t + 1, n_s, 6, length), jnp.float32),
                pltpu.VMEM((n_t, n_s, 6, length), jnp.float32),
                pltpu.VMEM((n_s, 6, length), jnp.float32),
                pltpu.VMEM((2, 6) + rows, jnp.float32),
                pltpu.VMEM((total, total // CLUSTER), jnp.bfloat16),
                dma((n_s,)), dma((n_s,)),
                dma((n_s,)), dma((n_s,)),
                dma((n_s,)), dma((n_s,)),
                dma((n_t,)), dma((n_t,)),
                dma((n_s,)), dma((n_s,)),
                dma, dma,
            ],
            compiler_params=pltpu.CompilerParams(collective_id=0, has_side_effects=True),
        )(start_state, fine_nodes.reshape(-1, lanes))
        nodes, ends = (1, 3, 3, length), (1, 3, length)
        return tuple(
            one.reshape(shape) for one, shape in zip(results, (nodes, nodes, ends, ends))
        )

    return jax.shard_map(
        shards,
        mesh=mesh,
        in_specs=(P(None, "space"), P("tm", None, None, "space")),
        out_specs=(
            P("tm", None, None, "space"),
            P("tm", None, None, "space"),
            P("tm", None, "space"),
            P("tm", None, "space"),
        ),
        check_vma=False,
    )
```
